32 devices in a mesh: dp: 4 (over z), owner: 2 (over x), tensor: 4 (over y, core).
Axes of the slice: x: 2, y: 2, z: 4, core: 2. Of those that a mesh axis runs over, the one named last changes fastest.
Arguments:
- train_act: bfloat16 [8, 512, 8192], P(('dp', 'owner'), None, 'tensor'), may hold values from -6 to 6
- train_grad: bfloat16 [8, 512, 28672], P(('dp', 'owner'), None, 'tensor'), may hold values from -0.0234375 to 0.0234375
- query_act: bfloat16 [8, 128, 8192], P(('dp', 'owner'), None, 'tensor'), may hold values from -6 to 6
- query_grad: bfloat16 [8, 128, 28672], P(('dp', 'owner'), None, 'tensor'), may hold values from -0.0234375 to 0.0234375
- basis_out: bfloat16 [28672, 512], P('tensor', 'owner'), may hold values from -0.03125 to 0.03125
- basis_in: bfloat16 [8192, 512], P('tensor', 'owner'), may hold values from -0.0625 to 0.0625
- eigen_corr: float32 [512, 512], P('tensor'), may hold values from 0.05 to 5
- seq_lengths: int32 [8], P(('dp', 'owner')), may hold values from 1 to 512, as said below
- seq_buckets: int32 [8], P(('dp', 'owner')), may hold values from 0 to 3, as said below
Outputs:
- influence: float32 [8, 8], P(('dp', 'owner'))
The draws below stay inside these ranges and needn't reach their ends.
Inputs may be any that keep to these rules, and one draw needn't show every extreme that they name: `seq_lengths`: some sequence has exactly 512 real tokens. (seq_buckets[n] + 1) * 128 >= seq_lengths[n]; bucket 0 and bucket 3 (the last) both occur.
All inputs are finite; a program needn't handle non-finite values.
Results may differ from the reference program's by a relative error of at most 0.008.
Values may be sent and summed in bfloat16 or wider, within the bound.
No kernel may reach another device: no remote copies, remote signals or barrier semaphores. Data moves between devices by JAX's collectives and lax.ppermute only.
A program may use at most 128 MiB of HBM per device.

```python
import math
import jax
import jax.numpy as jnp
from jax import lax

D = 8192
FF = 28672
RANK = 512
LEN = 512
NBUCK = 4
QLEN = 128
NSEQ = 8
NQ = 8


def draw_joint(key):
    base_key = jax.random.fold_in(key, 11)
    subkeys = jax.random.split(base_key, 5)
    bucket_span = LEN // NBUCK
    lengths = jax.random.randint(subkeys[0], (NSEQ,), 1, LEN + 1, dtype=jnp.int32)
    longest = jax.random.randint(subkeys[1], (), 0, NSEQ, dtype=jnp.int32)
    shortest = (longest + 1 + jax.random.randint(subkeys[2], (), 0, NSEQ - 1, dtype=jnp.int32)) % NSEQ
    short_len = jax.random.randint(subkeys[3], (), 1, bucket_span + 1, dtype=jnp.int32)
    lengths = lengths.at[longest].set(LEN).at[shortest].set(short_len)
    bump_up = jax.random.randint(subkeys[4], (NSEQ,), 0, 2, dtype=jnp.int32)
    bump_up = bump_up.at[shortest].set(0)
    buckets = jnp.minimum((lengths - 1) // bucket_span + bump_up, NBUCK - 1)
    return (lengths, buckets)


def draw_seq_lengths(key, part):
    return draw_joint(key)[0]


def draw_seq_buckets(key, part):
    return draw_joint(key)[1]


def level_of(own_key, shape, shards, least, largest):
    def one(axis_at, shards_of):
        heights = jax.random.uniform(jax.random.fold_in(jax.random.fold_in(own_key, 6), axis_at), (shards_of,), jnp.float32, least / len(shards), largest / len(shards))
        return jnp.repeat(jnp.exp(heights), shape[axis_at] // shards_of).reshape((-1,) + (1,) * (len(shape) - axis_at - 1))

    loudness = one(*shards[0])
    for cut in shards[1:]:
        loudness = loudness * one(*cut)
    return loudness


def noise(rng, dims, width, bound, pieces=(), kind=jnp.bfloat16):
    drawn = width * jax.random.normal(rng, dims, jnp.float32)
    if pieces:
        drawn = drawn * level_of(rng, dims, pieces, -0.22, 0.18)
    return jnp.clip(drawn, -bound, bound).astype(kind)


def setup_inputs(seed: int = 0) -> dict:
    streams_of = jax.random.split(jax.random.key(seed), 10)
    train_act = noise(streams_of[0], (NSEQ, LEN, D), 1.0, 6.0, ((0, 8), (2, 4)))
    train_grad = noise(streams_of[1], (NSEQ, LEN, FF), 0.004, 0.0234375, ((0, 8), (2, 4)))
    query_act = noise(streams_of[2], (NQ, QLEN, D), 1.0, 6.0, ((0, 8), (2, 4)))
    query_grad = noise(streams_of[3], (NQ, QLEN, FF), 0.004, 0.0234375, ((0, 8), (2, 4)))
    basis_out = noise(streams_of[4], (FF, RANK), FF ** -0.5, 0.03125, ((0, 4), (1, 2)))
    basis_in = noise(streams_of[5], (D, RANK), D ** -0.5, 0.0625, ((0, 4), (1, 2)))
    eigen_corr = jnp.clip(jnp.exp(math.log(5.0) - 4.6051702 * jax.random.uniform(streams_of[6], (RANK, RANK), jnp.float32) ** level_of(streams_of[6], (RANK, RANK), ((0, 4),), -0.2, 0.2)), 0.05, 5.0)
    seq_lengths = draw_seq_lengths(jax.random.fold_in(streams_of[9], 71), 0)
    seq_buckets = draw_seq_buckets(jax.random.fold_in(streams_of[9], 71), 0)
    return {"train_act": train_act, "train_grad": train_grad, "query_act": query_act, "query_grad": query_grad, "basis_out": basis_out, "basis_in": basis_in, "eigen_corr": eigen_corr, "seq_lengths": seq_lengths, "seq_buckets": seq_buckets}


damping = 0.05


def rotate_rows(gradients, activations, basis_out, basis_in):
    rotated_out = jnp.dot(gradients, basis_out, preferred_element_type=jnp.float32).astype(jnp.bfloat16)
    rotated_in = jnp.dot(activations, basis_in, preferred_element_type=jnp.float32).astype(jnp.bfloat16)
    return rotated_out, rotated_in


def reference(train_act, train_grad, query_act, query_grad, basis_out, basis_in, eigen_corr, seq_lengths, seq_buckets):
    bucket_span = LEN // NBUCK
    positions = jnp.arange(LEN, dtype=jnp.int32)

    def train_panel(record):
        activations, gradients, length, bucket = record
        rotated_out, rotated_in = rotate_rows(gradients, activations, basis_out, basis_in)
        bucket_end = (bucket + 1) * bucket_span
        live_mask = (positions >= bucket_end - length) & (positions < bucket_end)
        masked = rotated_out * live_mask.astype(rotated_out.dtype)[:, None]
        return jnp.dot(masked.T, rotated_in, preferred_element_type=jnp.float32).astype(jnp.bfloat16)

    def query_panel(record):
        activations, gradients = record
        rotated_out, rotated_in = rotate_rows(gradients, activations, basis_out, basis_in)
        return jnp.dot(rotated_out.T, rotated_in, preferred_element_type=jnp.float32)

    train_rot = lax.map(train_panel, (train_act, train_grad, seq_lengths, seq_buckets))
    query_rot = lax.map(query_panel, (query_act, query_grad))
    precond = query_rot / (eigen_corr + damping)
    return jnp.einsum("nij,qij->nq", train_rot.astype(jnp.float32), precond, precision=lax.Precision.HIGHEST)
```

```python
import jax
import jax.numpy as jnp
from jax import lax
from jax.experimental import pallas as pl
from jax.experimental.pallas import tpu as pltpu
from jax.sharding import PartitionSpec as P


LEN = 512
NBUCK = 4
damping = 0.05
PARITY, PLACE, OWNER, BEGIN, END, HERE = range(6)


def block_of(depth):
    return next(b for b in (1792, 1024, 512, 256, depth) if depth % b == 0)


def flip(array, axis, mask):
    size = lax.axis_size(axis)
    return lax.ppermute(array, axis, [(i, i ^ mask) for i in range(size)])


def cut(where, basis, size, spans):
    block = min(block_of(size), 512)
    width = basis.shape[1]

    def body(where_ref, *refs):
        for source, target in zip(refs[: len(spans)], refs[len(spans) :]):
            target[...] = source[...]

    def span(first, added):
        return lambda k, where_ref: (first // block + where_ref[PARITY] * (added // block) + k, 0)

    return pl.pallas_call(
        body,
        out_shape=[jax.ShapeDtypeStruct((size, width), basis.dtype) for _ in spans],
        grid_spec=pltpu.PrefetchScalarGridSpec(
            num_scalar_prefetch=1,
            grid=(size // block,),
            in_specs=[pl.BlockSpec((block, width), span(*s)) for s in spans],
            out_specs=[pl.BlockSpec((block, width), lambda k, where_ref: (k, 0)) for _ in spans],
        ),
    )(where, *[basis] * len(spans))


def rotate_own(act, qact, basis_in, grad, qgrad, basis_out):
    total, qtotal, half = grad.shape[0], qgrad.shape[0], basis_in.shape[1]
    deep = block_of(basis_out.shape[0])
    steps = basis_out.shape[0] // deep
    shallow = basis_in.shape[0] // steps

    def body(a, qa, bi, g, qg, bo, out_ref):
        @pl.when(pl.program_id(0) == 0)
        def _():
            out_ref[...] = jnp.zeros_like(out_ref)

        for rows, qrows, piece, cols in ((a, qa, bi, slice(0, half)), (g, qg, bo, slice(half, 2 * half))):
            held = piece[...]
            out_ref[:total, cols] += jnp.dot(rows[...], held, preferred_element_type=jnp.float32)
            out_ref[total:, cols] += jnp.dot(qrows[...], held, preferred_element_type=jnp.float32)

    def specs(block):
        return [
            pl.BlockSpec((total, block), lambda k: (0, k)),
            pl.BlockSpec((qtotal, block), lambda k: (0, k)),
            pl.BlockSpec((block, half), lambda k: (k, 0)),
        ]

    depth = basis_in.shape[0] + basis_out.shape[0]
    return pl.pallas_call(
        body,
        out_shape=jax.ShapeDtypeStruct((total + qtotal, 2 * half), jnp.float32),
        grid=(steps,),
        in_specs=specs(shallow) + specs(deep),
        out_specs=pl.BlockSpec((total + qtotal, 2 * half), lambda k: (0, 0)),
        cost_estimate=pl.CostEstimate(
            flops=2 * (total + qtotal) * half * depth, bytes_accessed=2 * depth * (total + qtotal + half), transcendentals=0
        ),
    )(act, qact, basis_in, grad, qgrad, basis_out)


def rotate(where, rows, qrows, parts, acc=None, ways=None):
    pieces = [piece for piece, _, _ in parts]
    count, cols, depth = len(pieces), pieces[0].shape[1], pieces[0].shape[0]
    block = min(block_of(depth), 512)
    steps = depth // block
    total, qtotal = rows.shape[0], qrows.shape[0]
    height = total + qtotal

    def body(where_ref, *refs):
        rows_refs, qrows_refs = refs[:count], refs[count : 2 * count]
        piece_refs = refs[2 * count : 3 * count]
        out_ref = refs[-1] if ways else refs[3 * count + (acc is not None)]

        @pl.when(pl.program_id(0) == 0)
        def _():
            out_ref[...] = jnp.zeros_like(out_ref) if acc is None else refs[3 * count][...]

        for n in range(count):
            piece = piece_refs[n][...]
            out_ref[:total, :] += jnp.dot(rows_refs[n][...], piece, preferred_element_type=jnp.float32)
            out_ref[total:, :] += jnp.dot(qrows_refs[n][...], piece, preferred_element_type=jnp.float32)

        if ways:

            @pl.when(pl.program_id(0) == steps - 1)
            def _():
                outs = refs[3 * count + (acc is not None) : -1]
                outs[0][...] = out_ref[:total, :]
                share = qtotal // ways
                for k in range(ways):
                    begin = pl.multiple_of(total + (where_ref[PLACE] ^ k) * share, share)
                    outs[1 + k][...] = out_ref[pl.ds(begin, share), :]

    def span(n):
        _, first, added = parts[n]
        return lambda k, where_ref: (0, first // block + where_ref[PARITY] * (added // block) + k)

    def whole(shape):
        return pl.BlockSpec(shape, lambda k, where_ref: (0, 0))

    in_specs = [pl.BlockSpec((total, block), span(n)) for n in range(count)]
    in_specs += [pl.BlockSpec((qtotal, block), span(n)) for n in range(count)]
    in_specs += [pl.BlockSpec((block, cols), lambda k, where_ref: (k, 0)) for _ in range(count)]
    operands = [rows] * count + [qrows] * count + pieces
    if acc is not None:
        in_specs.append(whole((height, cols)))
        operands.append(acc)
    shapes, scratch = [(height, cols)], []
    if ways:
        shapes = [(total, cols)] + [(qtotal // ways, cols)] * ways
        scratch = [pltpu.VMEM((height, cols), jnp.float32)]
    outs = pl.pallas_call(
        body,
        out_shape=[jax.ShapeDtypeStruct(shape, jnp.float32) for shape in shapes],
        grid_spec=pltpu.PrefetchScalarGridSpec(
            num_scalar_prefetch=1,
            grid=(steps,),
            in_specs=in_specs,
            out_specs=[whole(shape) for shape in shapes],
            scratch_shapes=scratch,
        ),
        cost_estimate=pl.CostEstimate(
            flops=2 * height * cols * depth * count,
            bytes_accessed=2 * count * depth * (height + cols) + 8 * height * cols,
            transcendentals=0,
        ),
    )(where, *operands)
    return outs if ways else outs[0]


def weigh(where, own, inner, outer, query, corr):
    length, half = outer[0].shape
    places, share, _ = query[0].shape
    rows = places * share
    blocks, tall = len(corr), corr[0].shape[0]

    def body(where_ref, own_a, own_b, in_a, in_b, out_a, out_b, qa, qb, *refs):
        corr_refs, (far_ref, near_ref, part_ref), curv = refs[:blocks], refs[blocks:-1], refs[-1]
        side, begin, end = where_ref[OWNER], where_ref[BEGIN], where_ref[END]
        for k in range(blocks):
            curv[pl.ds(pl.multiple_of((where_ref[PLACE] ^ k) * tall, tall), tall), :] = corr_refs[k][...]

        def rounded(a, b, cols):
            return (a[:length, cols] + b[:length, cols].astype(jnp.float32)).astype(jnp.bfloat16)

        everything, first, second = slice(None), slice(0, half), slice(half, 2 * half)
        ins = (rounded(own_a, own_b, first), rounded(in_a, in_b, everything))
        outs = (rounded(own_a, own_b, second), rounded(out_a, out_b, everything))
        position = lax.broadcasted_iota(jnp.int32, (length, half), 0)
        live = ((position >= begin) & (position < end)).astype(jnp.bfloat16)
        near = qa[...].reshape(rows, 3 * half)
        far = qb[...].reshape(rows, 3 * half)
        qins = (
            jnp.concatenate([near[:, :half], far[:, 2 * half :]], 0),
            jnp.concatenate([near[:, 2 * half :], far[:, :half]], 0),
        )
        moved = []
        for h in range(2):
            masked = outs[h] * live
            total = jnp.zeros((2 * rows, half), jnp.float32)
            for j in range(2):
                rot = lax.dot_general(
                    masked, ins[j], (((0,), (0,)), ((), ())), preferred_element_type=jnp.float32
                )
                rot = rot.astype(jnp.bfloat16).astype(jnp.float32)
                weight = rot / (
                    curv[
                        pl.ds(pl.multiple_of((side ^ h) * half, half), half),
                        pl.ds(pl.multiple_of((side ^ j) * half, half), half),
                    ]
                    + damping
                )
                high = weight.astype(jnp.bfloat16)
                low = (weight - high.astype(jnp.float32)).astype(jnp.bfloat16)
                for part in (high, low):
                    total += lax.dot_general(
                        qins[j], part, (((1,), (1,)), ((), ())), preferred_element_type=jnp.float32
                    )
            moved.append(total)
        near_ref[...] = moved[1][:rows]
        far_ref[...] = moved[0][rows:]
        part_ref[:places, :] = row_sums(moved[0][:rows] * near[:, half : 2 * half].astype(jnp.float32), places)
        part_ref[places:, :] = row_sums(moved[1][rows:] * far[:, half : 2 * half].astype(jnp.float32), places)

    vmem = pl.BlockSpec(memory_space=pltpu.VMEM)
    product = jax.ShapeDtypeStruct((rows, half), jnp.float32)
    return pl.pallas_call(
        body,
        out_shape=[product, product, jax.ShapeDtypeStruct((2 * places, half), jnp.float32)],
        in_specs=[pl.BlockSpec(memory_space=pltpu.SMEM)] + [vmem] * (8 + blocks),
        out_specs=[vmem] * 3,
        scratch_shapes=[pltpu.VMEM((blocks * tall, corr[0].shape[1]), jnp.float32)],
    )(where, *own, *inner, *outer, *query, *corr)


def row_sums(values, places):
    rows, width = values.shape
    return jnp.sum(values.reshape(places, rows // places, width), axis=1)


def gather_scores(where, moved, late, masks):
    far, near, part = moved
    places, share, half = late[0].shape
    count = 2 * places

    def body(where_ref, far_ref, near_ref, part_ref, la, lb, out_ref):
        def met(product, block):
            return row_sums(product[...] * block[...].reshape(places * share, half).astype(jnp.float32), places)

        sums = part_ref[...] + jnp.concatenate([met(near_ref, la), met(far_ref, lb)], 0)
        sums = jnp.sum(sums, axis=1, keepdims=True)
        index = lax.broadcasted_iota(jnp.int32, (count, 128), 0)
        query = jnp.zeros((count, 128), jnp.int32)
        for n, mask in enumerate(masks):
            query = jnp.where(index == n, mask, query)
        query = query ^ where_ref[HERE]
        hits = lax.broadcasted_iota(jnp.int32, (count, 128), 1) == query
        line = jnp.sum(jnp.where(hits, sums, 0.0), axis=0, keepdims=True)
        out_ref[...] = jnp.broadcast_to(line, out_ref.shape)

    vmem = pl.BlockSpec(memory_space=pltpu.VMEM)
    return pl.pallas_call(
        body,
        out_shape=jax.ShapeDtypeStruct((8, 128), jnp.float32),
        in_specs=[pl.BlockSpec(memory_space=pltpu.SMEM)] + [vmem] * 5,
        out_specs=vmem,
    )(where, far, near, part, *late)


def on_device(
    train_act,
    train_grad,
    query_act,
    query_grad,
    basis_out,
    basis_in,
    eigen_corr,
    seq_lengths,
    seq_buckets,
):
    dp, owner, place = lax.axis_index("dp"), lax.axis_index("owner"), lax.axis_index("tensor")
    tensor_size, dp_size = lax.axis_size("tensor"), lax.axis_size("dp")
    grad, act = train_grad[0], train_act[0]
    qgrad, qact = query_grad[0], query_act[0]
    length, qlength = grad.shape[0], qgrad.shape[0]
    share = qlength // tensor_size
    parity = dp % 2
    bf16, f32 = jnp.bfloat16, jnp.float32
    bits = [1 << n for n in range(tensor_size.bit_length() - 1)]

    ends = (seq_buckets[0] + 1) * (LEN // NBUCK)
    here = dp * lax.axis_size("owner") + owner
    where = jnp.stack([parity, place, owner, ends - seq_lengths[0], ends, here]).astype(jnp.int32)

    width_in, width_out = basis_in.shape[0], basis_out.shape[0]
    step = width_out // 7

    def fetch(mine, base, size):
        direct = flip(mine, "owner", 1)
        relayed = flip(direct, "dp", 1)
        return (direct, base, size), (relayed, base + size, -size)

    first = lax.dynamic_slice_in_dim(basis_in, parity * (width_in // 2), width_in // 2, 0)
    in_parts = fetch(first, 0, width_in // 2)
    spans = [(2 * n * step, step) for n in range(3)] + [(6 * step, 0)]
    shares = [*cut(where, basis_out, step, spans[:1])]
    *later, last = cut(where, basis_out, step, spans[1:])
    shares += later
    chunks = [fetch(shares[n], 2 * n * step, step) for n in range(3)]
    last = (flip(last, "owner", 1), 6 * step, 0)

    def shared(value):
        for bit in bits[:-1]:
            value = value + flip(value, "tensor", bit)
        return value, flip(value.astype(bf16), "tensor", bits[-1])

    own = rotate_own(act, qact, basis_in, grad, qgrad, basis_out)
    own = shared(own)
    inner = rotate(where, act, qact, in_parts)
    inner = shared(inner)

    corr = [eigen_corr]
    for k in range(1, tensor_size):
        corr.append(flip(eigen_corr, "tensor", k))

    groups = []
    bit = 1
    while bit < dp_size:
        ways = min(4, dp_size // bit)
        groups.append([("dp", bit * k, bit * k * lax.axis_size("owner")) for k in range(1, ways)])
        bit *= ways
    groups.append([("owner", 1, 1)])

    def everyone(block):
        gathered = block[None]
        for group in groups:
            peers = []
            for axis, mask, _ in group:
                peers.append(flip(gathered, axis, mask))
            if group is groups[-1]:
                return gathered, peers[0]
            gathered = jnp.concatenate([gathered, *peers], 0)

    masks = [0]
    for group in groups:
        masks = [m ^ added for added in [0] + [g for _, _, g in group] for m in masks]

    def my_rows(pair):
        a, b = (lax.dynamic_slice_in_dim(v, length + place * share, share, 0) for v in pair)
        return (a + b.astype(f32)).astype(bf16)

    early = everyone(jnp.concatenate([my_rows(own), my_rows(inner)], 1))

    acc = None
    for parts in (chunks[0], chunks[1], [chunks[2][0], last]):
        acc = rotate(where, grad, qgrad, parts, acc)
    outer, *qouter = rotate(where, grad, qgrad, [chunks[2][1]], acc, ways=tensor_size)
    qsum = qouter[0]
    for k in range(1, tensor_size):
        qsum = qsum + flip(qouter[k], "tensor", k)
    late = everyone(qsum.astype(bf16))
    outer = shared(outer)

    moved = weigh(where, own, inner, outer, early, corr)
    scores = gather_scores(where, moved, late, masks)
    pieces = [scores]
    for k in range(1, tensor_size):
        pieces.append(flip(scores, "tensor", k))
    while len(pieces) > 1:
        pieces = [a + b for a, b in zip(pieces[::2], pieces[1::2])]
    return pieces[0][:1, : 2 * late[0].shape[0]]


def solution(mesh):
    return jax.shard_map(
        on_device,
        mesh=mesh,
        in_specs=(
            P(("dp", "owner"), None, "tensor"),
            P(("dp", "owner"), None, "tensor"),
            P(("dp", "owner"), None, "tensor"),
            P(("dp", "owner"), None, "tensor"),
            P("tensor", "owner"),
            P("tensor", "owner"),
            P("tensor", None),
            P(("dp", "owner")),
            P(("dp", "owner")),
        ),
        out_specs=P(("dp", "owner"), None),
        check_vma=False,
    )
```

```python
import jax
import jax.numpy as jnp
from jax import lax
from jax.experimental import pallas as pl
from jax.experimental.pallas import tpu as pltpu
from jax.sharding import PartitionSpec as P


LEN = 512
NBUCK = 4
damping = 0.05
PARITY, PLACE, OWNER, BEGIN, END, HERE = range(6)


def block_of(depth):
    return next(b for b in (1792, 1024, 512, 256, depth) if depth % b == 0)


def flip(array, axis, mask):
    size = lax.axis_size(axis)
    return lax.ppermute(array, axis, [(i, i ^ mask) for i in range(size)])


def cut(where, basis, size, spans):
    block = min(block_of(size), 512)
    width = basis.shape[1]

    def body(where_ref, *refs):
        for source, target in zip(refs[: len(spans)], refs[len(spans) :]):
            target[...] = source[...]

    def span(first, added):
        return lambda k, where_ref: (first // block + where_ref[PARITY] * (added // block) + k, 0)

    return pl.pallas_call(
        body,
        out_shape=[jax.ShapeDtypeStruct((size, width), basis.dtype) for _ in spans],
        grid_spec=pltpu.PrefetchScalarGridSpec(
            num_scalar_prefetch=1,
            grid=(size // block,),
            in_specs=[pl.BlockSpec((block, width), span(*s)) for s in spans],
            out_specs=[pl.BlockSpec((block, width), lambda k, where_ref: (k, 0)) for _ in spans],
        ),
    )(where, *[basis] * len(spans))


def rotate_own(act, qact, basis_in, grad, qgrad, basis_out):
    total, qtotal, half = grad.shape[0], qgrad.shape[0], basis_in.shape[1]
    deep = block_of(basis_out.shape[0])
    steps = basis_out.shape[0] // deep
    shallow = basis_in.shape[0] // steps

    def body(a, qa, bi, g, qg, bo, out_ref):
        @pl.when(pl.program_id(0) == 0)
        def _():
            out_ref[...] = jnp.zeros_like(out_ref)

        for rows, qrows, piece, cols in ((a, qa, bi, slice(0, half)), (g, qg, bo, slice(half, 2 * half))):
            held = piece[...]
            out_ref[:total, cols] += jnp.dot(rows[...], held, preferred_element_type=jnp.float32)
            out_ref[total:, cols] += jnp.dot(qrows[...], held, preferred_element_type=jnp.float32)

    def specs(block):
        return [
            pl.BlockSpec((total, block), lambda k: (0, k)),
            pl.BlockSpec((qtotal, block), lambda k: (0, k)),
            pl.BlockSpec((block, half), lambda k: (k, 0)),
        ]

    depth = basis_in.shape[0] + basis_out.shape[0]
    return pl.pallas_call(
        body,
        out_shape=jax.ShapeDtypeStruct((total + qtotal, 2 * half), jnp.float32),
        grid=(steps,),
        in_specs=specs(shallow) + specs(deep),
        out_specs=pl.BlockSpec((total + qtotal, 2 * half), lambda k: (0, 0)),
        cost_estimate=pl.CostEstimate(
            flops=2 * (total + qtotal) * half * depth, bytes_accessed=2 * depth * (total + qtotal + half), transcendentals=0
        ),
    )(act, qact, basis_in, grad, qgrad, basis_out)


def rotate(where, rows, qrows, parts, acc=None, ways=None):
    pieces = [piece for piece, _, _ in parts]
    count, cols, depth = len(pieces), pieces[0].shape[1], pieces[0].shape[0]
    block = min(block_of(depth), 512)
    steps = depth // block
    total, qtotal = rows.shape[0], qrows.shape[0]
    height = total + qtotal

    def body(where_ref, *refs):
        rows_refs, qrows_refs = refs[:count], refs[count : 2 * count]
        piece_refs = refs[2 * count : 3 * count]
        out_ref = refs[-1] if ways else refs[3 * count + (acc is not None)]

        @pl.when(pl.program_id(0) == 0)
        def _():
            out_ref[...] = jnp.zeros_like(out_ref) if acc is None else refs[3 * count][...]

        for n in range(count):
            piece = piece_refs[n][...]
            out_ref[:total, :] += jnp.dot(rows_refs[n][...], piece, preferred_element_type=jnp.float32)
            out_ref[total:, :] += jnp.dot(qrows_refs[n][...], piece, preferred_element_type=jnp.float32)

        if ways:

            @pl.when(pl.program_id(0) == steps - 1)
            def _():
                outs = refs[3 * count + (acc is not None) : -1]
                outs[0][...] = out_ref[:total, :]
                share = qtotal // ways
                for k in range(ways):
                    begin = pl.multiple_of(total + (where_ref[PLACE] ^ k) * share, share)
                    outs[1 + k][...] = out_ref[pl.ds(begin, share), :]

    def span(n):
        _, first, added = parts[n]
        return lambda k, where_ref: (0, first // block + where_ref[PARITY] * (added // block) + k)

    def whole(shape):
        return pl.BlockSpec(shape, lambda k, where_ref: (0, 0))

    in_specs = [pl.BlockSpec((total, block), span(n)) for n in range(count)]
    in_specs += [pl.BlockSpec((qtotal, block), span(n)) for n in range(count)]
    in_specs += [pl.BlockSpec((block, cols), lambda k, where_ref: (k, 0)) for _ in range(count)]
    operands = [rows] * count + [qrows] * count + pieces
    if acc is not None:
        in_specs.append(whole((height, cols)))
        operands.append(acc)
    shapes, scratch = [(height, cols)], []
    if ways:
        shapes = [(total, cols)] + [(qtotal // ways, cols)] * ways
        scratch = [pltpu.VMEM((height, cols), jnp.float32)]
    outs = pl.pallas_call(
        body,
        out_shape=[jax.ShapeDtypeStruct(shape, jnp.float32) for shape in shapes],
        grid_spec=pltpu.PrefetchScalarGridSpec(
            num_scalar_prefetch=1,
            grid=(steps,),
            in_specs=in_specs,
            out_specs=[whole(shape) for shape in shapes],
            scratch_shapes=scratch,
        ),
        cost_estimate=pl.CostEstimate(
            flops=2 * height * cols * depth * count,
            bytes_accessed=2 * count * depth * (height + cols) + 8 * height * cols,
            transcendentals=0,
        ),
    )(where, *operands)
    return outs if ways else outs[0]


def meet(rows, inputs, curvatures, queries):
    total = jnp.zeros((queries[0].shape[0], rows.shape[1]), jnp.float32)
    for given, curvature, query in zip(inputs, curvatures, queries):
        rot = lax.dot_general(rows, given, (((0,), (0,)), ((), ())), preferred_element_type=jnp.float32)
        weight = rot.astype(jnp.bfloat16).astype(jnp.float32) * curvature
        high = weight.astype(jnp.bfloat16)
        low = (weight - high.astype(jnp.float32)).astype(jnp.bfloat16)
        for part in (high, low):
            total += lax.dot_general(
                query, part, (((1,), (1,)), ((), ())), preferred_element_type=jnp.float32
            )
    return total


def live_rows(where_ref, shape):
    position = lax.broadcasted_iota(jnp.int32, shape, 0)
    return ((position >= where_ref[BEGIN]) & (position < where_ref[END])).astype(jnp.bfloat16)


def weigh_own(where, length, own, inner, query, corr):
    half = inner[0].shape[1]
    places, share, _ = query[0].shape
    rows = places * share
    blocks, tall = len(corr), corr[0].shape[0]

    def body(where_ref, own_a, own_b, in_a, in_b, qa, qb, *refs):
        corr_refs, (far_ref, part_ref, ins_ref, qins_ref, curv_ref, curv) = refs[:blocks], refs[blocks:]
        side = where_ref[OWNER]
        for k in range(blocks):
            curv[pl.ds(pl.multiple_of((where_ref[PLACE] ^ k) * tall, tall), tall), :] = corr_refs[k][...]

        def rounded(a, b, cols):
            return (a[:length, cols] + b[:length, cols].astype(jnp.float32)).astype(jnp.bfloat16)

        def inverse(i, j):
            return 1.0 / (
                curv[
                    pl.ds(pl.multiple_of((side ^ i) * half, half), half),
                    pl.ds(pl.multiple_of((side ^ j) * half, half), half),
                ]
                + damping
            )

        everything, first, second = slice(None), slice(0, half), slice(half, 2 * half)
        ins = (rounded(own_a, own_b, first), rounded(in_a, in_b, everything))
        near = qa[...].reshape(rows, 3 * half)
        far = qb[...].reshape(rows, 3 * half)
        qins = (
            jnp.concatenate([near[:, :half], far[:, 2 * half :]], 0),
            jnp.concatenate([near[:, 2 * half :], far[:, :half]], 0),
        )
        masked = rounded(own_a, own_b, second) * live_rows(where_ref, (length, half))
        total = meet(masked, ins, [inverse(0, 0), inverse(0, 1)], qins)
        far_ref[...] = total[rows:]
        part_ref[...] = row_sums(total[:rows] * near[:, half : 2 * half].astype(jnp.float32), places)
        for j in range(2):
            ins_ref[j] = ins[j]
            qins_ref[j] = qins[j]
            curv_ref[j] = inverse(1, j)

    vmem = pl.BlockSpec(memory_space=pltpu.VMEM)
    return pl.pallas_call(
        body,
        out_shape=[
            jax.ShapeDtypeStruct((rows, half), jnp.float32),
            jax.ShapeDtypeStruct((places, half), jnp.float32),
            jax.ShapeDtypeStruct((2, length, half), jnp.bfloat16),
            jax.ShapeDtypeStruct((2, 2 * rows, half), jnp.bfloat16),
            jax.ShapeDtypeStruct((2, half, half), jnp.float32),
        ],
        in_specs=[pl.BlockSpec(memory_space=pltpu.SMEM)] + [vmem] * (6 + blocks),
        out_specs=[vmem] * 5,
        scratch_shapes=[pltpu.VMEM((blocks * tall, corr[0].shape[1]), jnp.float32)],
    )(where, *own, *inner, *query, *corr)


def weigh_other(where, outer, ins, qins, curvature, far):
    length, half = outer[0].shape
    places, share, _ = far.shape
    rows = places * share

    def body(where_ref, out_a, out_b, ins_ref, qins_ref, curv_ref, far_ref, near_ref, part_ref):
        rounded = (out_a[...] + out_b[...].astype(jnp.float32)).astype(jnp.bfloat16)
        masked = rounded * live_rows(where_ref, (length, half))
        total = meet(masked, [ins_ref[j] for j in range(2)], [curv_ref[j] for j in range(2)], [qins_ref[j] for j in range(2)])
        near_ref[...] = total[:rows]
        theirs = far_ref[...].reshape(rows, 3 * half)[:, half : 2 * half]
        part_ref[...] = row_sums(total[rows:] * theirs.astype(jnp.float32), places)

    vmem = pl.BlockSpec(memory_space=pltpu.VMEM)
    return pl.pallas_call(
        body,
        out_shape=[jax.ShapeDtypeStruct((rows, half), jnp.float32), jax.ShapeDtypeStruct((places, half), jnp.float32)],
        in_specs=[pl.BlockSpec(memory_space=pltpu.SMEM)] + [vmem] * 6,
        out_specs=[vmem] * 2,
    )(where, *outer, ins, qins, curvature, far)


def row_sums(values, places):
    rows, width = values.shape
    return jnp.sum(values.reshape(places, rows // places, width), axis=1)


def gather_scores(where, moved, late, masks):
    places, share, half = late[0].shape
    count = 2 * places

    def body(where_ref, far_ref, part_a, near_ref, part_b, la, lb, out_ref):
        def met(product, block):
            return row_sums(product[...] * block[...].reshape(places * share, half).astype(jnp.float32), places)

        sums = jnp.concatenate([part_a[...] + met(near_ref, la), part_b[...] + met(far_ref, lb)], 0)
        sums = jnp.sum(sums, axis=1, keepdims=True)
        index = lax.broadcasted_iota(jnp.int32, (count, 128), 0)
        query = jnp.zeros((count, 128), jnp.int32)
        for n, mask in enumerate(masks):
            query = jnp.where(index == n, mask, query)
        query = query ^ where_ref[HERE]
        hits = lax.broadcasted_iota(jnp.int32, (count, 128), 1) == query
        line = jnp.sum(jnp.where(hits, sums, 0.0), axis=0, keepdims=True)
        out_ref[...] = jnp.broadcast_to(line, out_ref.shape)

    vmem = pl.BlockSpec(memory_space=pltpu.VMEM)
    return pl.pallas_call(
        body,
        out_shape=jax.ShapeDtypeStruct((8, 128), jnp.float32),
        in_specs=[pl.BlockSpec(memory_space=pltpu.SMEM)] + [vmem] * 6,
        out_specs=vmem,
    )(where, *moved, *late)


def on_device(
    train_act,
    train_grad,
    query_act,
    query_grad,
    basis_out,
    basis_in,
    eigen_corr,
    seq_lengths,
    seq_buckets,
):
    dp, owner, place = lax.axis_index("dp"), lax.axis_index("owner"), lax.axis_index("tensor")
    tensor_size, dp_size = lax.axis_size("tensor"), lax.axis_size("dp")
    grad, act = train_grad[0], train_act[0]
    qgrad, qact = query_grad[0], query_act[0]
    length, qlength = grad.shape[0], qgrad.shape[0]
    share = qlength // tensor_size
    parity = dp % 2
    bf16, f32 = jnp.bfloat16, jnp.float32
    bits = [1 << n for n in range(tensor_size.bit_length() - 1)]

    ends = (seq_buckets[0] + 1) * (LEN // NBUCK)
    here = dp * lax.axis_size("owner") + owner
    where = jnp.stack([parity, place, owner, ends - seq_lengths[0], ends, here]).astype(jnp.int32)

    width_in, width_out = basis_in.shape[0], basis_out.shape[0]
    step = width_out // 7

    def fetch(mine, base, size):
        direct = flip(mine, "owner", 1)
        relayed = flip(direct, "dp", 1)
        return (direct, base, size), (relayed, base + size, -size)

    first = lax.dynamic_slice_in_dim(basis_in, parity * (width_in // 2), width_in // 2, 0)
    in_parts = fetch(first, 0, width_in // 2)
    spans = [(2 * n * step, step) for n in range(3)] + [(6 * step, 0)]
    shares = [*cut(where, basis_out, step, spans[:1])]
    *later, last = cut(where, basis_out, step, spans[1:])
    shares += later
    chunks = [fetch(shares[n], 2 * n * step, step) for n in range(3)]
    last = (flip(last, "owner", 1), 6 * step, 0)

    def shared(value):
        for bit in bits[:-1]:
            value = value + flip(value, "tensor", bit)
        return value, flip(value.astype(bf16), "tensor", bits[-1])

    own = rotate_own(act, qact, basis_in, grad, qgrad, basis_out)
    own = shared(own)
    inner = rotate(where, act, qact, in_parts)
    inner = shared(inner)

    corr = [eigen_corr]
    for k in range(1, tensor_size):
        corr.append(flip(eigen_corr, "tensor", k))

    groups = []
    bit = 1
    while bit < dp_size:
        ways = min(4, dp_size // bit)
        groups.append([("dp", bit * k, bit * k * lax.axis_size("owner")) for k in range(1, ways)])
        bit *= ways
    groups.append([("owner", 1, 1)])

    def everyone(block):
        gathered = block[None]
        for group in groups:
            peers = []
            for axis, mask, _ in group:
                peers.append(flip(gathered, axis, mask))
            if group is groups[-1]:
                return gathered, peers[0]
            gathered = jnp.concatenate([gathered, *peers], 0)

    masks = [0]
    for group in groups:
        masks = [m ^ added for added in [0] + [g for _, _, g in group] for m in masks]

    def my_rows(pair):
        a, b = (lax.dynamic_slice_in_dim(v, length + place * share, share, 0) for v in pair)
        return (a + b.astype(f32)).astype(bf16)

    early = everyone(jnp.concatenate([my_rows(own), my_rows(inner)], 1))

    acc = None
    for parts in (chunks[0], chunks[1], [chunks[2][0], last]):
        acc = rotate(where, grad, qgrad, parts, acc)
    outer, *qouter = rotate(where, grad, qgrad, [chunks[2][1]], acc, ways=tensor_size)
    qsum = qouter[0]
    for k in range(1, tensor_size):
        qsum = qsum + flip(qouter[k], "tensor", k)
    late = everyone(qsum.astype(bf16))
    outer = shared(outer)

    far, own_part, *kept = weigh_own(where, length, own, inner, early, corr)
    near, other_part = weigh_other(where, outer, *kept, early[1])
    moved = (far, own_part, near, other_part)
    scores = gather_scores(where, moved, late, masks)
    pieces = [scores]
    for k in range(1, tensor_size):
        pieces.append(flip(scores, "tensor", k))
    while len(pieces) > 1:
        pieces = [a + b for a, b in zip(pieces[::2], pieces[1::2])]
    return pieces[0][:1, : 2 * late[0].shape[0]]


def solution(mesh):
    return jax.shard_map(
        on_device,
        mesh=mesh,
        in_specs=(
            P(("dp", "owner"), None, "tensor"),
            P(("dp", "owner"), None, "tensor"),
            P(("dp", "owner"), None, "tensor"),
            P(("dp", "owner"), None, "tensor"),
            P("tensor", "owner"),
            P("tensor", "owner"),
            P("tensor", None),
            P(("dp", "owner")),
            P(("dp", "owner")),
        ),
        out_specs=P(("dp", "owner"), None),
        check_vma=False,
    )
```
